32 devices in a mesh: groups: 2 (over y), tensor: 16 (over z, x, core).
Axes of the slice: x: 2, y: 2, z: 4, core: 2. Of those that a mesh axis runs over, the one named last changes fastest.
Arguments:
- tokens: bfloat16 [64, 8192], P(('groups', 'tensor')), parts along dimension 0, may hold values from -6 to 6
- out_grad: bfloat16 [64, 8192], P(('groups', 'tensor')), parts along dimension 0, may hold values from -6 to 6
- w_gate: bfloat16 [8192, 16384], P(None, 'tensor'), may hold values from -0.0625 to 0.0625
- w_up: bfloat16 [8192, 16384], P(None, 'tensor'), may hold values from -0.0625 to 0.0625
- w_down: bfloat16 [16384, 8192], P('tensor'), may hold values from -0.046875 to 0.046875
- deltas: bfloat16 [6, 64, 128, 128], P('groups', 'tensor'), parts along dimension 0, may hold values from -0.1875 to 0.1875
- model_block: int32 [6, 64], P('groups', 'tensor'), parts along dimension 0, may hold values from 0 to 63
- hidden_block: int32 [6, 64], P('groups', 'tensor'), parts along dimension 0, may hold values from 0 to 127, as said below
- live_count: int32 [6, 16], P('groups', 'tensor'), parts along dimension 0, may hold values from 1 to 4
- prior_mean: float32 [6, 64, 128, 128], P('groups', 'tensor'), parts along dimension 0, may hold values from -6 to 6
- prior_square: float32 [6, 64, 128, 128], P('groups', 'tensor'), parts along dimension 0, may hold values from 0.01 to 1
Outputs:
- input_grad: bfloat16 [64, 8192], P(('groups', 'tensor')), parts along dimension 0
- moment_mean: float32 [6, 64, 128, 128], P('groups', 'tensor'), parts along dimension 0
- moment_square: float32 [6, 64, 128, 128], P('groups', 'tensor'), parts along dimension 0
The draws below stay inside these ranges and needn't reach their ends.
There are 2 independent parts, one for each index of `groups`. The reference program is written for one: setup_inputs(seed, part) draws one part's arguments, and reference() takes and returns one part's arrays. A program takes and returns all parts, laid end to end along the dimension named above; an argument that names none is the same for every part. Nothing has to cross between parts.
Inputs may be any that keep to these rules, and one draw needn't show every extreme that they name: `hidden_block`: the slots s of index j of tensor (j * 4 <= s < (j + 1) * 4) lie in hidden blocks j * 8 to (j + 1) * 8 - 1.
All inputs are finite; a program needn't handle non-finite values.
Results may differ from the reference program's by a relative error of at most 0.005.
Values may be sent and summed in bfloat16 or wider, within the bound.
No kernel may reach another device: no remote copies, remote signals or barrier semaphores. Data moves between devices by JAX's collectives and lax.ppermute only.
A program may use at most 128 MiB of HBM per device.

```python
import math
import jax
import jax.numpy as jnp

D = 8192
FF = 16384
BS = 128
NB_DEV = 4
TOKENS = 32
NBLK = 64
CB = 8
N_TENSOR = 16


def draw_hidden_block(key, part):
    slot_index = jnp.arange(NBLK)
    owner = slot_index // NB_DEV
    offset = jax.random.randint(key, (3, NBLK), 0, CB)
    offset = jnp.where(slot_index[None, :] == 0, 0, offset)
    offset = jnp.where(slot_index[None, :] == NBLK - 1, CB - 1, offset)
    return (owner[None, :] * CB + offset).astype(jnp.int32)


def draw_model_block(key, part):
    keys = jax.random.split(key, 3)
    rows = [jax.random.permutation(keys[0], NBLK) % (D // BS), jax.random.permutation(keys[1], NBLK) % (D // BS), jax.random.permutation(keys[2], NBLK) % (D // BS)]
    return jnp.stack(rows).astype(jnp.int32)


def draw_live_count(key, part):
    devices = NBLK // NB_DEV
    keys = jax.random.split(key, 3)
    counts = jax.random.randint(keys[0], (3, devices), 1, NB_DEV + 1)
    fullest = jax.random.randint(keys[1], (3,), 0, devices)
    emptiest = (fullest + 1 + jax.random.randint(keys[2], (3,), 0, devices - 1)) % devices
    places = jnp.arange(devices)
    counts = jnp.where(places[None, :] == fullest[:, None], NB_DEV, counts)
    counts = jnp.where(places[None, :] == emptiest[:, None], 1, counts)
    return counts.astype(jnp.int32)


def level_of(own_key, extent, pieces, low, largest):
    def one(position, blocks):
        heights = jax.random.uniform(jax.random.fold_in(jax.random.fold_in(own_key, 6), position), (blocks,), jnp.float32, low / len(pieces), largest / len(pieces))
        return jnp.repeat(jnp.exp(heights), extent[position] // blocks).reshape((-1,) + (1,) * (len(extent) - position - 1))

    factor_of = one(*pieces[0])
    for cut in pieces[1:]:
        factor_of = factor_of * one(*cut)
    return factor_of


def centred(rng, shape, width, limit, pieces=(), held_as=jnp.bfloat16):
    result = jax.random.normal(rng, shape, jnp.float32) * width
    if len(pieces) > 0:
        result = level_of(rng, shape, pieces, -0.22, 0.18) * result
    return jnp.clip(result, min=-limit, max=limit).astype(held_as)


def setup_inputs(seed: int = 0, part: int = 0) -> dict:
    streams_of = jax.random.split(jax.random.key(seed), 12)
    part_keys = jax.random.split(jax.random.fold_in(streams_of[11], part), 12)
    return {
        "tokens": centred(part_keys[0], (TOKENS, D), 1.0, 6.0, ((0, 16),)),
        "out_grad": centred(part_keys[1], (TOKENS, D), 1.0, 6.0, ((0, 16),)),
        "w_gate": centred(streams_of[2], (D, FF), D ** -0.5, 0.0625, ((1, 16),)),
        "w_up": centred(streams_of[3], (D, FF), D ** -0.5, 0.0625, ((1, 16),)),
        "w_down": centred(streams_of[4], (FF, D), FF ** -0.5, 0.046875, ((0, 16),)),
        "deltas": centred(part_keys[5], (3, NBLK, BS, BS), 1024 ** -0.5, 0.1875, ((1, 16),)),
        "model_block": draw_model_block(jax.random.fold_in(jax.random.fold_in(streams_of[11], part), 71), part),
        "hidden_block": draw_hidden_block(jax.random.fold_in(jax.random.fold_in(streams_of[11], part), 71), part),
        "live_count": draw_live_count(jax.random.fold_in(jax.random.fold_in(streams_of[11], part), 71), part),
        "prior_mean": centred(part_keys[9], (3, NBLK, BS, BS), 1.0, 6.0, ((1, 16),), jnp.float32),
        "prior_square": jnp.clip(jnp.exp(math.log(1.0) - 4.6051702 * jax.random.uniform(part_keys[10], (3, NBLK, BS, BS), jnp.float32) ** level_of(part_keys[10], (3, NBLK, BS, BS), ((1, 16),), -0.2, 0.2)), 0.01, 1.0),
    }


def pick(values, index):
    count = values.shape[0]
    return jnp.take(values.reshape(count, -1, BS), index, axis=1)


def place(contrib, index, columns):
    count = contrib.shape[0]
    empty = jnp.zeros((count, columns, BS), jnp.float32)
    return empty.at[:, index].add(contrib).reshape(count, columns * BS)


def activate(gate_pre, up_pre, grad_act):
    sigma = jax.nn.sigmoid(gate_pre)
    silu_gate = gate_pre * sigma
    activ = (silu_gate * up_pre).astype(jnp.bfloat16)
    grad_up = (grad_act * silu_gate).astype(jnp.bfloat16)
    grad_gate = (grad_act * up_pre * sigma * (1.0 + gate_pre * (1.0 - sigma))).astype(jnp.bfloat16)
    return activ, grad_up, grad_gate


def reference(tokens, out_grad, w_gate, w_up, w_down, deltas, model_block, hidden_block, live_count, prior_mean, prior_square):
    slots = deltas.shape[1]
    per_device = slots // N_TENSOR
    owner = (jnp.arange(slots) // per_device).astype(jnp.int32)
    within = jnp.arange(slots) % per_device
    live = within[None, :] < live_count[:, owner]
    active = jnp.where(live[:, :, None, None], deltas, jnp.zeros_like(deltas)).astype(jnp.float32)
    model_cols = D // BS
    hidden_cols = FF // BS
    picked_gate = pick(tokens, model_block[0]).astype(jnp.float32)
    picked_up = pick(tokens, model_block[1]).astype(jnp.float32)
    picked_down = pick(out_grad, model_block[2]).astype(jnp.float32)
    gate_pre = jnp.dot(tokens, w_gate, preferred_element_type=jnp.float32) + place(
        jnp.einsum("tsk,skj->tsj", picked_gate, active[0]), hidden_block[0], hidden_cols)
    up_pre = jnp.dot(tokens, w_up, preferred_element_type=jnp.float32) + place(
        jnp.einsum("tsk,skj->tsj", picked_up, active[1]), hidden_block[1], hidden_cols)
    grad_act = jnp.dot(out_grad, w_down.T, preferred_element_type=jnp.float32) + place(
        jnp.einsum("tsk,sjk->tsj", picked_down, active[2]), hidden_block[2], hidden_cols)
    activ, grad_up, grad_gate = activate(gate_pre, up_pre, grad_act)
    gate_hidden = pick(grad_gate, hidden_block[0]).astype(jnp.float32)
    up_hidden = pick(grad_up, hidden_block[1]).astype(jnp.float32)
    act_hidden = pick(activ, hidden_block[2]).astype(jnp.float32)
    dense = jnp.dot(grad_gate, w_gate.T, preferred_element_type=jnp.float32) + jnp.dot(grad_up, w_up.T, preferred_element_type=jnp.float32)
    back_gate = place(jnp.einsum("tsj,skj->tsk", gate_hidden, active[0]), model_block[0], model_cols)
    back_up = place(jnp.einsum("tsj,skj->tsk", up_hidden, active[1]), model_block[1], model_cols)
    input_grad = (dense + back_gate + back_up).astype(jnp.bfloat16)
    block_gate = jnp.einsum("tsk,tsj->skj", picked_gate, gate_hidden)
    block_up = jnp.einsum("tsk,tsj->skj", picked_up, up_hidden)
    block_down = jnp.einsum("tsk,tsj->skj", act_hidden, picked_down)
    grads = jnp.stack([block_gate, block_up, block_down])
    keep = live[:, :, None, None]
    moment_mean = jnp.where(keep, 0.9 * prior_mean + 0.1 * grads, prior_mean)
    moment_square = jnp.where(keep, 0.999 * prior_square + 0.001 * grads * grads, prior_square)
    return input_grad, moment_mean, moment_square
```

```python
import functools

import jax
import jax.numpy as jnp
from jax import lax
from jax.experimental import pallas as pl
from jax.experimental.pallas import tpu as pltpu
from jax.sharding import PartitionSpec as P

BS = 128
MIB = 1 << 20
ROW_BY_ROW = (((1,), (1,)), ((), ()))
BY_TOKEN = (((0,), (0,)), ((), ()))
VMEM = pl.BlockSpec(memory_space=pltpu.VMEM)
SMEM = pl.BlockSpec(memory_space=pltpu.SMEM)
HBM = pl.BlockSpec(memory_space=pltpu.HBM)


def dot(a, b, dims=(((1,), (0,)), ((), ()))):
    return lax.dot_general(a, b, dims, preferred_element_type=jnp.float32)


def load_kernel(start, chunks, w_hbm, out_ref, sem):
    rows = out_ref.shape[0] // chunks
    copies = [
        pltpu.make_async_copy(
            w_hbm.at[pl.ds(start + i * rows, rows)],
            out_ref.at[pl.ds(i * rows, rows)],
            sem.at[i],
        )
        for i in range(chunks)
    ]
    for copy in copies:
        copy.start()
    for copy in copies:
        copy.wait()


def in_hbm(value):
    return pltpu.with_memory_space_constraint(value, pltpu.HBM)


def load(weight, start, rows):
    chunks = 4
    return pl.pallas_call(
        functools.partial(load_kernel, start, chunks),
        out_shape=pltpu.VMEM((rows, weight.shape[1]), weight.dtype),
        in_specs=[HBM],
        out_specs=VMEM,
        scratch_shapes=[pltpu.SemaphoreType.DMA((chunks,))],
        compiler_params=pltpu.CompilerParams(vmem_limit_bytes=MIB),
    )(in_hbm(weight))


def forward_kernel(
    width, mine, theirs, g_lo, g_hi, u_lo, u_hi, w_down, deltas, model, hidden, live,
    rows_ref, activ_ref, up_ref, gate_ref, gate_acc, up_acc, act_acc, d_buf, sem,
):
    half = mine.shape[0]
    slots = deltas.shape[1]
    blocks = gate_ref.shape[1] // BS
    step = w_down.shape[0] // sem.shape[0]
    copies = [
        pltpu.make_async_copy(
            w_down.at[pl.ds(i * step, step)], d_buf.at[pl.ds(i * step, step)], sem.at[i]
        )
        for i in range(sem.shape[0])
    ]
    for copy in copies:
        copy.start()
    rows_ref[0:half, :] = mine[...]
    rows_ref[half : 2 * half, :] = theirs[...]
    depth = g_lo.shape[0]
    gate_acc[...] = dot(rows_ref[:, 0:depth], g_lo[...])
    gate_acc[...] += dot(rows_ref[:, depth:width], g_hi[...])
    up_acc[...] = dot(rows_ref[:, 0:depth], u_lo[...])
    up_acc[...] += dot(rows_ref[:, depth:width], u_hi[...])
    for copy in copies:
        copy.wait()
    act_acc[...] = dot(d_buf[...], rows_ref[:, width:], ROW_BY_ROW)
    grad_act = act_acc[...].T
    for m, acc in ((0, gate_acc), (1, up_acc)):
        for s in range(slots):

            @pl.when(s < live[m])
            def _(m=m, s=s, acc=acc):
                at_m = pl.ds(pl.multiple_of(model[m, s] * BS, BS), BS)
                at_h = pl.ds(pl.multiple_of(lax.rem(hidden[m, s], blocks) * BS, BS), BS)
                acc[:, at_h] += dot(rows_ref[:, at_m], deltas[m, s])

    gate_pre = gate_acc[...]
    up_pre = up_acc[...]
    gate_acc[...] = grad_act
    for s in range(slots):

        @pl.when(s < live[2])
        def _(s=s):
            at_m = pl.ds(pl.multiple_of(width + model[2, s] * BS, BS), BS)
            at_h = pl.ds(pl.multiple_of(lax.rem(hidden[2, s], blocks) * BS, BS), BS)
            gate_acc[:, at_h] += dot(rows_ref[:, at_m], deltas[2, s], ROW_BY_ROW)

    grad_act = gate_acc[...]
    sigma = jax.nn.sigmoid(gate_pre)
    silu_gate = gate_pre * sigma
    activ_ref[...] = (silu_gate * up_pre).astype(jnp.bfloat16)
    up_ref[...] = (grad_act * silu_gate).astype(jnp.bfloat16)
    gate_ref[...] = (grad_act * up_pre * sigma * (1.0 + gate_pre * (1.0 - sigma))).astype(
        jnp.bfloat16
    )


def backward_kernel(
    start, grad_gate, grad_up, g_part, u_part, deltas, model, hidden, live, keep_ref, send_ref, acc
):
    slots = deltas.shape[1]
    blocks = grad_gate.shape[1] // BS
    columns = g_part.shape[0]
    half = keep_ref.shape[0]
    total = dot(g_part[...], grad_gate[...], ROW_BY_ROW)
    total += dot(u_part[...], grad_up[...], ROW_BY_ROW)
    acc[...] = total.T
    for m, grad in ((0, grad_gate), (1, grad_up)):
        for s in range(slots):
            column = model[m, s] * BS - start

            @pl.when((s < live[m]) & (column >= 0) & (column < columns))
            def _(m=m, s=s, grad=grad, column=column):
                at_m = pl.ds(pl.multiple_of(column, BS), BS)
                at_h = pl.ds(pl.multiple_of(lax.rem(hidden[m, s], blocks) * BS, BS), BS)
                acc[:, at_m] += dot(grad[:, at_h], deltas[m, s], ROW_BY_ROW)

    keep_ref[...] = acc[0:half, :]
    send_ref[...] = acc[half:, :].astype(jnp.bfloat16)


def moments_kernel(
    width, rows, activ, grad_up, grad_gate, model, hidden, live, mean, square, mean_out, square_out
):
    slots = mean.shape[1]
    blocks = activ.shape[1] // BS
    for m, grad in ((0, grad_gate), (1, grad_up), (2, activ)):

        @pl.when(pl.program_id(0) == m)
        def _(m=m, grad=grad):
            for s in range(slots):
                at_h = pl.ds(pl.multiple_of(lax.rem(hidden[m, s], blocks) * BS, BS), BS)
                first = width if m == 2 else 0
                at_m = pl.ds(pl.multiple_of(first + model[m, s] * BS, BS), BS)
                if m == 2:
                    block = dot(grad[:, at_h], rows[:, at_m], BY_TOKEN)
                else:
                    block = dot(rows[:, at_m], grad[:, at_h], BY_TOKEN)
                keep = s < live[m]
                old_mean, old_square = mean[0, s], square[0, s]
                mean_out[0, s] = jnp.where(keep, 0.9 * old_mean + 0.1 * block, old_mean)
                square_out[0, s] = jnp.where(
                    keep, 0.999 * old_square + 0.001 * block * block, old_square
                )


def per_device(
    devices,
    tokens,
    out_grad,
    w_gate,
    w_up,
    w_down,
    deltas,
    model_block,
    hidden_block,
    live_count,
    prior_mean,
    prior_square,
):
    width, wide = w_gate.shape
    bits = [1 << k for k in range(devices.bit_length() - 1)]
    count = tokens.shape[0] * devices
    half = count // 2
    part = width // 2
    f32, bf16 = jnp.float32, jnp.bfloat16

    def swap(value, bit):
        return lax.ppermute(value, "tensor", [(i, i ^ bit) for i in range(devices)])

    live = live_count.reshape(-1)
    positions = (model_block, hidden_block, live)
    held = jnp.concatenate([tokens, out_grad], axis=1)
    for bit in bits[:0:-1]:
        came = swap(held, bit)
        held = jnp.concatenate([held, came], axis=0)
    other = swap(held, bits[0])
    g_parts = [load(w_gate, i * part, part) for i in range(2)]
    u_parts = [load(w_up, i * part, part) for i in range(2)]

    rows, activ, grad_up, grad_gate = pl.pallas_call(
        functools.partial(forward_kernel, width),
        out_shape=(
            jax.ShapeDtypeStruct((count, 2 * width), bf16),
            jax.ShapeDtypeStruct((count, wide), bf16),
            jax.ShapeDtypeStruct((count, wide), bf16),
            jax.ShapeDtypeStruct((count, wide), bf16),
        ),
        in_specs=[VMEM] * 6 + [HBM, VMEM] + [SMEM] * 3,
        out_specs=[VMEM] * 4,
        scratch_shapes=[
            pltpu.VMEM((count, wide), f32),
            pltpu.VMEM((count, wide), f32),
            pltpu.VMEM((wide, count), f32),
            pltpu.VMEM((wide, width), bf16),
            pltpu.SemaphoreType.DMA((4,)),
        ],
        compiler_params=pltpu.CompilerParams(vmem_limit_bytes=19 * MIB),
        name="forward",
    )(held, other, *g_parts, *u_parts, in_hbm(w_down), deltas, *positions)

    pieces = []
    for i in range(2):
        keep, send = pl.pallas_call(
            functools.partial(backward_kernel, i * part),
            out_shape=(
                jax.ShapeDtypeStruct((half, part), f32),
                jax.ShapeDtypeStruct((half, part), bf16),
            ),
            in_specs=[VMEM] * 5 + [SMEM] * 3,
            out_specs=[VMEM] * 2,
            scratch_shapes=[pltpu.VMEM((count, part), f32)],
            compiler_params=pltpu.CompilerParams(vmem_limit_bytes=8 * MIB),
        )(grad_gate, grad_up, g_parts[i], u_parts[i], deltas, *positions)
        left = half
        for bit in bits[:-1]:
            total = keep + swap(send, bit).astype(f32)
            left //= 2
            keep, send = total[:left], total[left:].astype(bf16)
        pieces.append((keep + swap(send, bits[-1]).astype(f32)).astype(bf16))
    input_grad = jnp.concatenate(pieces, axis=1)

    slots = deltas.shape[1]
    block = pl.BlockSpec((1, slots, BS, BS), lambda m: (m, 0, 0, 0))
    mean, square = pl.pallas_call(
        functools.partial(moments_kernel, width),
        grid=(3,),
        out_shape=(
            jax.ShapeDtypeStruct(prior_mean.shape, f32),
            jax.ShapeDtypeStruct(prior_square.shape, f32),
        ),
        in_specs=[VMEM] * 4 + [SMEM] * 3 + [block] * 2,
        out_specs=[block] * 2,
        compiler_params=pltpu.CompilerParams(vmem_limit_bytes=8 * MIB),
        name="moments",
    )(rows, activ, grad_up, grad_gate, *positions, prior_mean, prior_square)
    return input_grad, mean, square


def solution(mesh):
    placed = (
        P(("groups", "tensor"), None),
        P(("groups", "tensor"), None),
        P(None, "tensor"),
        P(None, "tensor"),
        P("tensor", None),
        P("groups", "tensor", None, None),
        P("groups", "tensor"),
        P("groups", "tensor"),
        P("groups", "tensor"),
        P("groups", "tensor", None, None),
        P("groups", "tensor", None, None),
    )
    devices = mesh.shape["tensor"]
    return jax.shard_map(
        functools.partial(per_device, devices),
        mesh=mesh,
        in_specs=placed,
        out_specs=(
            P(("groups", "tensor"), None),
            P("groups", "tensor", None, None),
            P("groups", "tensor", None, None),
        ),
        check_vma=False,
    )
```

```python
import functools

import jax
import jax.numpy as jnp
from jax import lax
from jax.experimental import pallas as pl
from jax.experimental.pallas import tpu as pltpu
from jax.sharding import PartitionSpec as P

BS = 128
MIB = 1 << 20
ROW_BY_ROW = (((1,), (1,)), ((), ()))
BY_TOKEN = (((0,), (0,)), ((), ()))
VMEM = pl.BlockSpec(memory_space=pltpu.VMEM)
SMEM = pl.BlockSpec(memory_space=pltpu.SMEM)
HBM = pl.BlockSpec(memory_space=pltpu.HBM)


def dot(a, b, dims=(((1,), (0,)), ((), ()))):
    return lax.dot_general(a, b, dims, preferred_element_type=jnp.float32)


def load_kernel(start, w_hbm, out_ref, sem):
    copy, _ = start_copies(w_hbm, start, out_ref, sem)

    def finish(i, carry):
        copy(i).wait()
        return carry

    lax.fori_loop(0, sem.shape[0], finish, 0)


def in_hbm(value):
    return pltpu.with_memory_space_constraint(value, pltpu.HBM)


def load(weight, start, rows):
    chunks = 2
    return pl.pallas_call(
        functools.partial(load_kernel, start),
        out_shape=pltpu.VMEM((rows, weight.shape[1]), weight.dtype),
        in_specs=[HBM],
        out_specs=VMEM,
        scratch_shapes=[pltpu.SemaphoreType.DMA((chunks,))],
        compiler_params=pltpu.CompilerParams(vmem_limit_bytes=MIB),
    )(in_hbm(weight))


def add_blocks(acc, source, deltas, m, model, hidden, live, transposed):
    blocks = acc.shape[1] // BS
    for s in range(deltas.shape[1]):
        at_m = pl.ds(pl.multiple_of(model[m, s] * BS, BS), BS)
        at_h = pl.ds(pl.multiple_of(lax.rem(hidden[m, s], blocks) * BS, BS), BS)
        active = jnp.where(s < live[m], deltas[m, s], jnp.zeros_like(deltas[m, s]))
        if transposed:
            acc[:, at_h] += dot(source[:, at_m], active, ROW_BY_ROW)
        else:
            acc[:, at_h] += dot(source[:, at_m], active)


def start_copies(source, start, target, sem):
    step = target.shape[0] // sem.shape[0]

    def copy(i):
        at = pl.multiple_of(i * step, step)
        return pltpu.make_async_copy(
            source.at[pl.ds(start + at, step)], target.at[pl.ds(at, step)], sem.at[i]
        )

    def begin(i, carry):
        copy(i).start()
        return carry

    lax.fori_loop(0, sem.shape[0], begin, 0)
    return copy, step


def forward_kernel(
    mine, theirs, g_lo, g_hi, u_lo, u_hi, w_down, deltas, model, hidden, live,
    x_ref, dy_ref, activ_ref, up_ref, gate_ref, gate_acc, up_acc, act_acc, d_part, sem,
):
    copy, step = start_copies(w_down, 0, d_part, sem)
    half, width = mine.shape[0], x_ref.shape[1]
    depth = g_lo.shape[0]
    x_ref[0:half, :] = mine[:, 0:width]
    x_ref[half:, :] = theirs[:, 0:width]
    dy_ref[0:half, :] = mine[:, width:]
    dy_ref[half:, :] = theirs[:, width:]
    gate_acc[...] = dot(x_ref[:, 0:depth], g_lo[...])
    gate_acc[...] += dot(x_ref[:, depth:], g_hi[...])
    up_acc[...] = dot(x_ref[:, 0:depth], u_lo[...])
    up_acc[...] += dot(x_ref[:, depth:], u_hi[...])
    add_blocks(gate_acc, x_ref, deltas, 0, model, hidden, live, False)
    add_blocks(up_acc, x_ref, deltas, 1, model, hidden, live, False)

    def down(i, carry):
        copy(i).wait()
        at = pl.ds(pl.multiple_of(i * step, step), step)
        act_acc[:, at] = dot(d_part[at, :], dy_ref[...], ROW_BY_ROW).T
        return carry

    lax.fori_loop(0, sem.shape[0], down, 0)
    add_blocks(act_acc, dy_ref, deltas, 2, model, hidden, live, True)
    gate, up, grad_act = gate_acc[...], up_acc[...], act_acc[...]
    sigma = jax.nn.sigmoid(gate)
    silu_gate = gate * sigma
    activ_ref[...] = (silu_gate * up).astype(jnp.bfloat16)
    up_ref[...] = (grad_act * silu_gate).astype(jnp.bfloat16)
    gate_ref[...] = (grad_act * up * sigma * (1.0 + gate * (1.0 - sigma))).astype(jnp.bfloat16)


def backward_kernel(
    start, grad_gate, grad_up, g_part, u_part, deltas, model, hidden, live, keep_ref, send_ref, acc
):
    slots = deltas.shape[1]
    blocks = grad_gate.shape[1] // BS
    columns = g_part.shape[0]
    half = keep_ref.shape[0]
    total = dot(g_part[...], grad_gate[...], ROW_BY_ROW)
    total += dot(u_part[...], grad_up[...], ROW_BY_ROW)
    acc[...] = total.T
    for m, grad in ((0, grad_gate), (1, grad_up)):
        for s in range(slots):
            column = model[m, s] * BS - start
            inside = (s < live[m]) & (column >= 0) & (column < columns)
            at_m = pl.ds(pl.multiple_of(jnp.clip(column, 0, columns - BS), BS), BS)
            at_h = pl.ds(pl.multiple_of(lax.rem(hidden[m, s], blocks) * BS, BS), BS)
            active = jnp.where(inside, deltas[m, s], jnp.zeros_like(deltas[m, s]))
            acc[:, at_m] += dot(grad[:, at_h], active, ROW_BY_ROW)

    keep_ref[...] = acc[0:half, :]
    send_ref[...] = acc[half:, :].astype(jnp.bfloat16)


def moments_kernel(
    x_rows, dy_rows, activ, grad_up, grad_gate, model, hidden, live, mean, square, mean_out, square_out
):
    slots = mean.shape[1]
    blocks = activ.shape[1] // BS
    for m, grad in ((0, grad_gate), (1, grad_up), (2, activ)):

        @pl.when(pl.program_id(0) == m)
        def _(m=m, grad=grad):
            for s in range(slots):
                at_h = pl.ds(pl.multiple_of(lax.rem(hidden[m, s], blocks) * BS, BS), BS)
                at_m = pl.ds(pl.multiple_of(model[m, s] * BS, BS), BS)
                if m == 2:
                    block = dot(grad[:, at_h], dy_rows[:, at_m], BY_TOKEN)
                else:
                    block = dot(x_rows[:, at_m], grad[:, at_h], BY_TOKEN)
                keep = s < live[m]
                old_mean, old_square = mean[0, s], square[0, s]
                mean_out[0, s] = jnp.where(keep, 0.9 * old_mean + 0.1 * block, old_mean)
                square_out[0, s] = jnp.where(
                    keep, 0.999 * old_square + 0.001 * block * block, old_square
                )


def stack(first, second, axis):
    zero = jnp.zeros((), first.dtype)
    after = [(0, 0, 0), (0, 0, 0)]
    before = [(0, 0, 0), (0, 0, 0)]
    after[axis] = (0, second.shape[axis], 0)
    before[axis] = (first.shape[axis], 0, 0)
    return lax.pad(first, zero, after) + lax.pad(second, zero, before)


def per_device(
    devices,
    tokens,
    out_grad,
    w_gate,
    w_up,
    w_down,
    deltas,
    model_block,
    hidden_block,
    live_count,
    prior_mean,
    prior_square,
):
    width, wide = w_gate.shape
    bits = [1 << k for k in range(devices.bit_length() - 1)]
    count = tokens.shape[0] * devices
    half = count // 2
    part = width // 2
    f32, bf16 = jnp.float32, jnp.bfloat16

    def swap(value, bit):
        return lax.ppermute(value, "tensor", [(i, i ^ bit) for i in range(devices)])

    live = live_count.reshape(-1)
    positions = (model_block, hidden_block, live)
    held = stack(tokens, out_grad, 1)
    for bit in bits[:0:-1]:
        held = stack(held, swap(held, bit), 0)
    other = swap(held, bits[0])
    g_parts = [load(w_gate, i * part, part) for i in range(2)]
    u_parts = [load(w_up, i * part, part) for i in range(2)]

    x_rows, dy_rows, activ, grad_up, grad_gate = pl.pallas_call(
        forward_kernel,
        out_shape=(
            jax.ShapeDtypeStruct((count, width), bf16),
            jax.ShapeDtypeStruct((count, width), bf16),
            jax.ShapeDtypeStruct((count, wide), bf16),
            jax.ShapeDtypeStruct((count, wide), bf16),
            jax.ShapeDtypeStruct((count, wide), bf16),
        ),
        in_specs=[VMEM] * 6 + [HBM, VMEM] + [SMEM] * 3,
        out_specs=[VMEM] * 5,
        scratch_shapes=[
            pltpu.VMEM((count, wide), f32),
            pltpu.VMEM((count, wide), f32),
            pltpu.VMEM((count, wide), f32),
            pltpu.VMEM(w_down.shape, bf16),
            pltpu.SemaphoreType.DMA((max(1, min(4, wide // BS)),)),
        ],
        compiler_params=pltpu.CompilerParams(vmem_limit_bytes=19 * MIB),
        name="forward",
    )(
        held, other, *g_parts, *u_parts, in_hbm(w_down), deltas, *positions
    )

    pieces = []
    for i in range(2):
        keep, send = pl.pallas_call(
            functools.partial(backward_kernel, i * part),
            out_shape=(
                jax.ShapeDtypeStruct((half, part), f32),
                jax.ShapeDtypeStruct((half, part), bf16),
            ),
            in_specs=[VMEM] * 5 + [SMEM] * 3,
            out_specs=[VMEM] * 2,
            scratch_shapes=[pltpu.VMEM((count, part), f32)],
            compiler_params=pltpu.CompilerParams(vmem_limit_bytes=8 * MIB),
        )(grad_gate, grad_up, g_parts[i], u_parts[i], deltas, *positions)
        pieces.append(keep + swap(send, bits[0]).astype(f32))
    left = half // 2
    keep = stack(pieces[0][:left], pieces[1][:left], 1)
    send = stack(pieces[0][left:], pieces[1][left:], 1).astype(bf16)
    for bit in bits[1:-1]:
        total = keep + swap(send, bit).astype(f32)
        left //= 2
        keep, send = total[:left], total[left:].astype(bf16)
    input_grad = (keep + swap(send, bits[-1]).astype(f32)).astype(bf16)

    slots = deltas.shape[1]
    block = pl.BlockSpec((1, slots, BS, BS), lambda m: (m, 0, 0, 0))
    mean, square = pl.pallas_call(
        moments_kernel,
        grid=(3,),
        out_shape=(
            jax.ShapeDtypeStruct(prior_mean.shape, f32),
            jax.ShapeDtypeStruct(prior_square.shape, f32),
        ),
        in_specs=[VMEM] * 5 + [SMEM] * 3 + [block] * 2,
        out_specs=[block] * 2,
        compiler_params=pltpu.CompilerParams(vmem_limit_bytes=8 * MIB),
        name="moments",
    )(x_rows, dy_rows, activ, grad_up, grad_gate, *positions, prior_mean, prior_square)
    return input_grad, mean, square


def solution(mesh):
    placed = (
        P(("groups", "tensor"), None),
        P(("groups", "tensor"), None),
        P(None, "tensor"),
        P(None, "tensor"),
        P("tensor", None),
        P("groups", "tensor", None, None),
        P("groups", "tensor"),
        P("groups", "tensor"),
        P("groups", "tensor"),
        P("groups", "tensor", None, None),
        P("groups", "tensor", None, None),
    )
    devices = mesh.shape["tensor"]
    return jax.shard_map(
        functools.partial(per_device, devices),
        mesh=mesh,
        in_specs=placed,
        out_specs=(
            P(("groups", "tensor"), None),
            P("groups", "tensor", None, None),
            P("groups", "tensor", None, None),
        ),
        check_vma=False,
    )
```

```python
import functools

import jax
import jax.numpy as jnp
from jax import lax
from jax.experimental import pallas as pl
from jax.experimental.pallas import tpu as pltpu
from jax.sharding import PartitionSpec as P

BS = 128
MIB = 1 << 20
ROW_BY_ROW = (((1,), (1,)), ((), ()))
BY_TOKEN = (((0,), (0,)), ((), ()))
VMEM = pl.BlockSpec(memory_space=pltpu.VMEM)
SMEM = pl.BlockSpec(memory_space=pltpu.SMEM)
HBM = pl.BlockSpec(memory_space=pltpu.HBM)


def dot(a, b, dims=(((1,), (0,)), ((), ()))):
    return lax.dot_general(a, b, dims, preferred_element_type=jnp.float32)


def load_kernel(start, w_hbm, out_ref, sem):
    copy, _ = start_copies(w_hbm, start, out_ref, sem)

    def finish(i, carry):
        copy(i).wait()
        return carry

    lax.fori_loop(0, sem.shape[0], finish, 0)


def in_hbm(value):
    return pltpu.with_memory_space_constraint(value, pltpu.HBM)


def load(weight, start, rows):
    chunks = 2
    return pl.pallas_call(
        functools.partial(load_kernel, start),
        out_shape=pltpu.VMEM((rows, weight.shape[1]), weight.dtype),
        in_specs=[HBM],
        out_specs=VMEM,
        scratch_shapes=[pltpu.SemaphoreType.DMA((chunks,))],
        compiler_params=pltpu.CompilerParams(vmem_limit_bytes=MIB),
    )(in_hbm(weight))


def add_blocks(acc, source, deltas, m, model, hidden, live, transposed):
    blocks = acc.shape[1] // BS
    for s in range(deltas.shape[1]):
        at_m = pl.ds(pl.multiple_of(model[m, s] * BS, BS), BS)
        at_h = pl.ds(pl.multiple_of(lax.rem(hidden[m, s], blocks) * BS, BS), BS)
        active = jnp.where(s < live[m], deltas[m, s], jnp.zeros_like(deltas[m, s]))
        if transposed:
            acc[:, at_h] += dot(source[:, at_m], active, ROW_BY_ROW)
        else:
            acc[:, at_h] += dot(source[:, at_m], active)


def start_copies(source, start, target, sem):
    step = target.shape[0] // sem.shape[0]

    def copy(i):
        at = pl.multiple_of(i * step, step)
        return pltpu.make_async_copy(
            source.at[pl.ds(start + at, step)], target.at[pl.ds(at, step)], sem.at[i]
        )

    def begin(i, carry):
        copy(i).start()
        return carry

    lax.fori_loop(0, sem.shape[0], begin, 0)
    return copy, step


def forward_kernel(
    mine, theirs, g_lo, g_hi, u_lo, w_up, w_down, deltas, model, hidden, live,
    x_ref, dy_ref, activ_ref, up_ref, gate_ref, u_hi, gate_acc, up_acc, act_acc, d_part, u_sem, sem,
):
    u_copy, _ = start_copies(w_up, w_up.shape[0] - u_hi.shape[0], u_hi, u_sem)
    copy, step = start_copies(w_down, 0, d_part, sem)
    half, width = mine.shape[0], x_ref.shape[1]
    depth = g_lo.shape[0]
    x_ref[0:half, :] = mine[:, 0:width]
    x_ref[half:, :] = theirs[:, 0:width]
    dy_ref[0:half, :] = mine[:, width:]
    dy_ref[half:, :] = theirs[:, width:]
    gate_acc[...] = dot(x_ref[:, 0:depth], g_lo[...])
    gate_acc[...] += dot(x_ref[:, depth:], g_hi[...])
    up_acc[...] = dot(x_ref[:, 0:depth], u_lo[...])
    for i in range(u_sem.shape[0]):
        u_copy(i).wait()
    up_acc[...] += dot(x_ref[:, depth:], u_hi[...])
    add_blocks(gate_acc, x_ref, deltas, 0, model, hidden, live, False)
    add_blocks(up_acc, x_ref, deltas, 1, model, hidden, live, False)

    def down(i, carry):
        copy(i).wait()
        at = pl.ds(pl.multiple_of(i * step, step), step)
        act_acc[:, at] = dot(d_part[at, :], dy_ref[...], ROW_BY_ROW).T
        return carry

    lax.fori_loop(0, sem.shape[0], down, 0)
    add_blocks(act_acc, dy_ref, deltas, 2, model, hidden, live, True)
    gate, up, grad_act = gate_acc[...], up_acc[...], act_acc[...]
    sigma = jax.nn.sigmoid(gate)
    silu_gate = gate * sigma
    activ_ref[...] = (silu_gate * up).astype(jnp.bfloat16)
    up_ref[...] = (grad_act * silu_gate).astype(jnp.bfloat16)
    gate_ref[...] = (grad_act * up * sigma * (1.0 + gate * (1.0 - sigma))).astype(jnp.bfloat16)


def backward_kernel(
    start, grad_gate, grad_up, g_part, u_part, deltas, model, hidden, live, keep_ref, send_ref, acc
):
    slots = deltas.shape[1]
    blocks = grad_gate.shape[1] // BS
    columns = g_part.shape[0]
    half = keep_ref.shape[0]
    tall = min(1024, columns)
    for i in range(0, columns, tall):
        total = dot(g_part[i : i + tall, :], grad_gate[...], ROW_BY_ROW)
        total += dot(u_part[i : i + tall, :], grad_up[...], ROW_BY_ROW)
        acc[:, i : i + tall] = total.T
    for m, grad in ((0, grad_gate), (1, grad_up)):
        for s in range(slots):
            column = model[m, s] * BS - start
            inside = (s < live[m]) & (column >= 0) & (column < columns)
            at_m = pl.ds(pl.multiple_of(jnp.clip(column, 0, columns - BS), BS), BS)
            at_h = pl.ds(pl.multiple_of(lax.rem(hidden[m, s], blocks) * BS, BS), BS)
            active = jnp.where(inside, deltas[m, s], jnp.zeros_like(deltas[m, s]))
            acc[:, at_m] += dot(grad[:, at_h], active, ROW_BY_ROW)

    keep_ref[...] = acc[0:half, :]
    send_ref[...] = acc[half:, :].astype(jnp.bfloat16)


def moments_kernel(
    x_rows, dy_rows, activ, grad_up, grad_gate, model, hidden, live, mean, square, mean_out, square_out
):
    slots = mean.shape[1]
    blocks = activ.shape[1] // BS
    for m, grad in ((0, grad_gate), (1, grad_up), (2, activ)):

        @pl.when(pl.program_id(0) == m)
        def _(m=m, grad=grad):
            for s in range(slots):
                at_h = pl.ds(pl.multiple_of(lax.rem(hidden[m, s], blocks) * BS, BS), BS)
                at_m = pl.ds(pl.multiple_of(model[m, s] * BS, BS), BS)
                if m == 2:
                    block = dot(grad[:, at_h], dy_rows[:, at_m], BY_TOKEN)
                else:
                    block = dot(x_rows[:, at_m], grad[:, at_h], BY_TOKEN)
                keep = s < live[m]
                old_mean, old_square = mean[0, s], square[0, s]
                mean_out[0, s] = jnp.where(keep, 0.9 * old_mean + 0.1 * block, old_mean)
                square_out[0, s] = jnp.where(
                    keep, 0.999 * old_square + 0.001 * block * block, old_square
                )


def stack(first, second, axis):
    zero = jnp.zeros((), first.dtype)
    after = [(0, 0, 0), (0, 0, 0)]
    before = [(0, 0, 0), (0, 0, 0)]
    after[axis] = (0, second.shape[axis], 0)
    before[axis] = (first.shape[axis], 0, 0)
    return lax.pad(first, zero, after) + lax.pad(second, zero, before)


def per_device(
    devices,
    tokens,
    out_grad,
    w_gate,
    w_up,
    w_down,
    deltas,
    model_block,
    hidden_block,
    live_count,
    prior_mean,
    prior_square,
):
    width, wide = w_gate.shape
    bits = [1 << k for k in range(devices.bit_length() - 1)]
    count = tokens.shape[0] * devices
    half = count // 2
    part = width // 2
    f32, bf16 = jnp.float32, jnp.bfloat16

    def swap(value, bit):
        return lax.ppermute(value, "tensor", [(i, i ^ bit) for i in range(devices)])

    live = live_count.reshape(-1)
    positions = (model_block, hidden_block, live)
    held = stack(tokens, out_grad, 1)
    for bit in bits[:0:-1]:
        held = stack(held, swap(held, bit), 0)
    other = swap(held, bits[0])
    g_parts = [load(w_gate, i * part, part) for i in range(2)]
    u_lo = load(w_up, 0, part)

    x_rows, dy_rows, activ, grad_up, grad_gate, u_hi = pl.pallas_call(
        forward_kernel,
        out_shape=(
            jax.ShapeDtypeStruct((count, width), bf16),
            jax.ShapeDtypeStruct((count, width), bf16),
            jax.ShapeDtypeStruct((count, wide), bf16),
            jax.ShapeDtypeStruct((count, wide), bf16),
            jax.ShapeDtypeStruct((count, wide), bf16),
            pltpu.VMEM((part, wide), bf16),
        ),
        in_specs=[VMEM] * 5 + [HBM, HBM, VMEM] + [SMEM] * 3,
        out_specs=[VMEM] * 6,
        scratch_shapes=[
            pltpu.VMEM((count, wide), f32),
            pltpu.VMEM((count, wide), f32),
            pltpu.VMEM((count, wide), f32),
            pltpu.VMEM(w_down.shape, bf16),
            pltpu.SemaphoreType.DMA((2,)),
            pltpu.SemaphoreType.DMA((max(1, min(4, wide // BS)),)),
        ],
        compiler_params=pltpu.CompilerParams(vmem_limit_bytes=19 * MIB),
        name="forward",
    )(
        held, other, *g_parts, u_lo, in_hbm(w_up), in_hbm(w_down), deltas, *positions
    )

    u_parts = (u_lo, u_hi)
    pieces = []
    for i in range(2):
        keep, send = pl.pallas_call(
            functools.partial(backward_kernel, i * part),
            out_shape=(
                jax.ShapeDtypeStruct((half, part), f32),
                jax.ShapeDtypeStruct((half, part), bf16),
            ),
            in_specs=[VMEM] * 5 + [SMEM] * 3,
            out_specs=[VMEM] * 2,
            scratch_shapes=[pltpu.VMEM((count, part), f32)],
            compiler_params=pltpu.CompilerParams(vmem_limit_bytes=8 * MIB),
        )(grad_gate, grad_up, g_parts[i], u_parts[i], deltas, *positions)
        pieces.append(keep + swap(send, bits[0]).astype(f32))
    left = half // 2
    keep = stack(pieces[0][:left], pieces[1][:left], 1)
    send = stack(pieces[0][left:], pieces[1][left:], 1).astype(bf16)
    for bit in bits[1:-1]:
        total = keep + swap(send, bit).astype(f32)
        left //= 2
        keep, send = total[:left], total[left:].astype(bf16)
    input_grad = (keep + swap(send, bits[-1]).astype(f32)).astype(bf16)

    slots = deltas.shape[1]
    block = pl.BlockSpec((1, slots, BS, BS), lambda m: (m, 0, 0, 0))
    mean, square = pl.pallas_call(
        moments_kernel,
        grid=(3,),
        out_shape=(
            jax.ShapeDtypeStruct(prior_mean.shape, f32),
            jax.ShapeDtypeStruct(prior_square.shape, f32),
        ),
        in_specs=[VMEM] * 5 + [SMEM] * 3 + [block] * 2,
        out_specs=[block] * 2,
        compiler_params=pltpu.CompilerParams(vmem_limit_bytes=8 * MIB),
        name="moments",
    )(x_rows, dy_rows, activ, grad_up, grad_gate, *positions, prior_mean, prior_square)
    return input_grad, mean, square


def solution(mesh):
    placed = (
        P(("groups", "tensor"), None),
        P(("groups", "tensor"), None),
        P(None, "tensor"),
        P(None, "tensor"),
        P("tensor", None),
        P("groups", "tensor", None, None),
        P("groups", "tensor"),
        P("groups", "tensor"),
        P("groups", "tensor"),
        P("groups", "tensor", None, None),
        P("groups", "tensor", None, None),
    )
    devices = mesh.shape["tensor"]
    return jax.shard_map(
        functools.partial(per_device, devices),
        mesh=mesh,
        in_specs=placed,
        out_specs=(
            P(("groups", "tensor"), None),
            P("groups", "tensor", None, None),
            P("groups", "tensor", None, None),
        ),
        check_vma=False,
    )
```

```python
import functools

import jax
import jax.numpy as jnp
from jax import lax
from jax.experimental import pallas as pl
from jax.experimental.pallas import tpu as pltpu
from jax.sharding import PartitionSpec as P

BS = 128
MIB = 1 << 20
ROW_BY_ROW = (((1,), (1,)), ((), ()))
BY_TOKEN = (((0,), (0,)), ((), ()))
VMEM = pl.BlockSpec(memory_space=pltpu.VMEM)
SMEM = pl.BlockSpec(memory_space=pltpu.SMEM)
HBM = pl.BlockSpec(memory_space=pltpu.HBM)


def dot(a, b, dims=(((1,), (0,)), ((), ()))):
    return lax.dot_general(a, b, dims, preferred_element_type=jnp.float32)


def load_kernel(start, w_hbm, out_ref, sem):
    copy, _ = start_copies(w_hbm, start, out_ref, sem)

    def finish(i, carry):
        copy(i).wait()
        return carry

    lax.fori_loop(0, sem.shape[0], finish, 0)


def in_hbm(value):
    return pltpu.with_memory_space_constraint(value, pltpu.HBM)


def load(weight, start, rows):
    chunks = 2
    return pl.pallas_call(
        functools.partial(load_kernel, start),
        out_shape=pltpu.VMEM((rows, weight.shape[1]), weight.dtype),
        in_specs=[HBM],
        out_specs=VMEM,
        scratch_shapes=[pltpu.SemaphoreType.DMA((chunks,))],
        compiler_params=pltpu.CompilerParams(vmem_limit_bytes=MIB),
    )(in_hbm(weight))


def add_blocks(acc, source, deltas, m, model, hidden, live, transposed):
    blocks = acc.shape[1] // BS
    for s in range(deltas.shape[1]):
        at_m = pl.ds(pl.multiple_of(model[m, s] * BS, BS), BS)
        at_h = pl.ds(pl.multiple_of(lax.rem(hidden[m, s], blocks) * BS, BS), BS)
        active = jnp.where(s < live[m], deltas[m, s], jnp.zeros_like(deltas[m, s]))
        if transposed:
            acc[:, at_h] += dot(source[:, at_m], active, ROW_BY_ROW)
        else:
            acc[:, at_h] += dot(source[:, at_m], active)


def start_copies(source, start, target, sem):
    step = target.shape[0] // sem.shape[0]

    def copy(i):
        at = pl.multiple_of(i * step, step)
        return pltpu.make_async_copy(
            source.at[pl.ds(start + at, step)], target.at[pl.ds(at, step)], sem.at[i]
        )

    def begin(i, carry):
        copy(i).start()
        return carry

    lax.fori_loop(0, sem.shape[0], begin, 0)
    return copy, step


def forward_kernel(
    mine, theirs, g_lo, g_hi, u_lo, w_up, w_down, deltas, model, hidden, live,
    x_ref, dy_ref, activ_ref, up_ref, gate_ref, u_hi, gate_acc, up_acc, act_acc, d_part, u_sem, sem,
):
    u_copy, _ = start_copies(w_up, w_up.shape[0] - u_hi.shape[0], u_hi, u_sem)
    copy, step = start_copies(w_down, 0, d_part, sem)
    half, width = mine.shape[0], x_ref.shape[1]
    depth = g_lo.shape[0]
    x_ref[0:half, :] = mine[:, 0:width]
    x_ref[half:, :] = theirs[:, 0:width]
    dy_ref[0:half, :] = mine[:, width:]
    dy_ref[half:, :] = theirs[:, width:]
    gate_acc[...] = dot(x_ref[:, 0:depth], g_lo[...])
    gate_acc[...] += dot(x_ref[:, depth:], g_hi[...])
    up_acc[...] = dot(x_ref[:, 0:depth], u_lo[...])
    for i in range(u_sem.shape[0]):
        u_copy(i).wait()
    up_acc[...] += dot(x_ref[:, depth:], u_hi[...])
    add_blocks(gate_acc, x_ref, deltas, 0, model, hidden, live, False)
    add_blocks(up_acc, x_ref, deltas, 1, model, hidden, live, False)

    def down(i, carry):
        copy(i).wait()
        at = pl.ds(pl.multiple_of(i * step, step), step)
        act_acc[:, at] = dot(d_part[at, :], dy_ref[...], ROW_BY_ROW).T
        return carry

    lax.fori_loop(0, sem.shape[0], down, 0)
    add_blocks(act_acc, dy_ref, deltas, 2, model, hidden, live, True)
    gate, up, grad_act = gate_acc[...], up_acc[...], act_acc[...]
    sigma = jax.nn.sigmoid(gate)
    silu_gate = gate * sigma
    activ_ref[...] = (silu_gate * up).astype(jnp.bfloat16)
    up_ref[...] = (grad_act * silu_gate).astype(jnp.bfloat16)
    gate_ref[...] = (grad_act * up * sigma * (1.0 + gate * (1.0 - sigma))).astype(jnp.bfloat16)


def backward_kernel(
    start, grad_gate, grad_up, g_part, u_part, deltas, model, hidden, live, keep_ref, send_ref, acc
):
    slots = deltas.shape[1]
    blocks = grad_gate.shape[1] // BS
    columns = g_part.shape[0]
    half = keep_ref.shape[0]
    tall = min(1024, columns)
    for i in range(0, columns, tall):
        total = dot(g_part[i : i + tall, :], grad_gate[...], ROW_BY_ROW)
        total += dot(u_part[i : i + tall, :], grad_up[...], ROW_BY_ROW)
        acc[:, i : i + tall] = total.T
    for m, grad in ((0, grad_gate), (1, grad_up)):
        for s in range(slots):
            column = model[m, s] * BS - start
            inside = (s < live[m]) & (column >= 0) & (column < columns)
            at_m = pl.ds(pl.multiple_of(jnp.clip(column, 0, columns - BS), BS), BS)
            at_h = pl.ds(pl.multiple_of(lax.rem(hidden[m, s], blocks) * BS, BS), BS)
            active = jnp.where(inside, deltas[m, s], jnp.zeros_like(deltas[m, s]))
            acc[:, at_m] += dot(grad[:, at_h], active, ROW_BY_ROW)

    keep_ref[...] = acc[0:half, :]
    send_ref[...] = acc[half:, :].astype(jnp.bfloat16)


def moments_kernel(
    x_rows, dy_rows, activ, grad_up, grad_gate, model, hidden, live, mean, square, mean_out, square_out
):
    slots = mean.shape[1]
    blocks = activ.shape[1] // BS
    for m, grad in ((0, grad_gate), (1, grad_up), (2, activ)):

        @pl.when(pl.program_id(0) == m)
        def _(m=m, grad=grad):
            for s in range(slots):
                at_h = pl.ds(pl.multiple_of(lax.rem(hidden[m, s], blocks) * BS, BS), BS)
                at_m = pl.ds(pl.multiple_of(model[m, s] * BS, BS), BS)
                if m == 2:
                    block = dot(grad[:, at_h], dy_rows[:, at_m], BY_TOKEN)
                else:
                    block = dot(x_rows[:, at_m], grad[:, at_h], BY_TOKEN)
                keep = s < live[m]
                old_mean, old_square = mean[0, s], square[0, s]
                mean_out[0, s] = jnp.where(keep, 0.9 * old_mean + 0.1 * block, old_mean)
                square_out[0, s] = jnp.where(
                    keep, 0.999 * old_square + 0.001 * block * block, old_square
                )


def stack(first, second, axis):
    zero = jnp.zeros((), first.dtype)
    after = [(0, 0, 0), (0, 0, 0)]
    before = [(0, 0, 0), (0, 0, 0)]
    after[axis] = (0, second.shape[axis], 0)
    before[axis] = (first.shape[axis], 0, 0)
    return lax.pad(first, zero, after) + lax.pad(second, zero, before)


def per_device(
    devices,
    tokens,
    out_grad,
    w_gate,
    w_up,
    w_down,
    deltas,
    model_block,
    hidden_block,
    live_count,
    prior_mean,
    prior_square,
):
    width, wide = w_gate.shape
    bits = [1 << k for k in range(devices.bit_length() - 1)]
    count = tokens.shape[0] * devices
    half = count // 2
    part = width // 2
    f32, bf16 = jnp.float32, jnp.bfloat16

    def swap(value, bit):
        return lax.ppermute(value, "tensor", [(i, i ^ bit) for i in range(devices)])

    live = live_count.reshape(-1)
    positions = (model_block, hidden_block, live)
    near, far = bits[:-2], bits[-2:]
    straight = [far[1], far[0], far[0] ^ far[1]]
    held = stack(tokens, out_grad, 1)
    came = [swap(held, bit) for bit in straight]
    held = stack(stack(held, came[0], 0), stack(came[1], came[2], 0), 0)
    for bit in near[:0:-1]:
        held = stack(held, swap(held, bit), 0)
    other = swap(held, bits[0])
    g_parts = [load(w_gate, i * part, part) for i in range(2)]
    u_lo = load(w_up, 0, part)

    x_rows, dy_rows, activ, grad_up, grad_gate, u_hi = pl.pallas_call(
        forward_kernel,
        out_shape=(
            jax.ShapeDtypeStruct((count, width), bf16),
            jax.ShapeDtypeStruct((count, width), bf16),
            jax.ShapeDtypeStruct((count, wide), bf16),
            jax.ShapeDtypeStruct((count, wide), bf16),
            jax.ShapeDtypeStruct((count, wide), bf16),
            pltpu.VMEM((part, wide), bf16),
        ),
        in_specs=[VMEM] * 5 + [HBM, HBM, VMEM] + [SMEM] * 3,
        out_specs=[VMEM] * 6,
        scratch_shapes=[
            pltpu.VMEM((count, wide), f32),
            pltpu.VMEM((count, wide), f32),
            pltpu.VMEM((count, wide), f32),
            pltpu.VMEM(w_down.shape, bf16),
            pltpu.SemaphoreType.DMA((2,)),
            pltpu.SemaphoreType.DMA((max(1, min(4, wide // BS)),)),
        ],
        compiler_params=pltpu.CompilerParams(vmem_limit_bytes=19 * MIB),
        name="forward",
    )(
        held, other, *g_parts, u_lo, in_hbm(w_up), in_hbm(w_down), deltas, *positions
    )

    u_parts = (u_lo, u_hi)
    pieces = []
    for i in range(2):
        keep, send = pl.pallas_call(
            functools.partial(backward_kernel, i * part),
            out_shape=(
                jax.ShapeDtypeStruct((half, part), f32),
                jax.ShapeDtypeStruct((half, part), bf16),
            ),
            in_specs=[VMEM] * 5 + [SMEM] * 3,
            out_specs=[VMEM] * 2,
            scratch_shapes=[pltpu.VMEM((count, part), f32)],
            compiler_params=pltpu.CompilerParams(vmem_limit_bytes=8 * MIB),
        )(grad_gate, grad_up, g_parts[i], u_parts[i], deltas, *positions)
        pieces.append(keep + swap(send, bits[0]).astype(f32))
    left = half // 2
    keep = stack(pieces[0][:left], pieces[1][:left], 1)
    send = stack(pieces[0][left:], pieces[1][left:], 1).astype(bf16)
    for bit in near[1:]:
        total = keep + swap(send, bit).astype(f32)
        left = total.shape[0] // 2
        keep, send = total[:left], total[left:].astype(bf16)
    rows = tokens.shape[0]
    input_grad = total[:rows]
    for k, bit in enumerate(straight, 1):
        send = total[k * rows : (k + 1) * rows].astype(bf16)
        input_grad += swap(send, bit).astype(f32)
    input_grad = input_grad.astype(bf16)

    slots = deltas.shape[1]
    block = pl.BlockSpec((1, slots, BS, BS), lambda m: (m, 0, 0, 0))
    mean, square = pl.pallas_call(
        moments_kernel,
        grid=(3,),
        out_shape=(
            jax.ShapeDtypeStruct(prior_mean.shape, f32),
            jax.ShapeDtypeStruct(prior_square.shape, f32),
        ),
        in_specs=[VMEM] * 5 + [SMEM] * 3 + [block] * 2,
        out_specs=[block] * 2,
        compiler_params=pltpu.CompilerParams(vmem_limit_bytes=8 * MIB),
        name="moments",
    )(x_rows, dy_rows, activ, grad_up, grad_gate, *positions, prior_mean, prior_square)
    return input_grad, mean, square


def solution(mesh):
    placed = (
        P(("groups", "tensor"), None),
        P(("groups", "tensor"), None),
        P(None, "tensor"),
        P(None, "tensor"),
        P("tensor", None),
        P("groups", "tensor", None, None),
        P("groups", "tensor"),
        P("groups", "tensor"),
        P("groups", "tensor"),
        P("groups", "tensor", None, None),
        P("groups", "tensor", None, None),
    )
    devices = mesh.shape["tensor"]
    return jax.shard_map(
        functools.partial(per_device, devices),
        mesh=mesh,
        in_specs=placed,
        out_specs=(
            P(("groups", "tensor"), None),
            P("groups", "tensor", None, None),
            P("groups", "tensor", None, None),
        ),
        check_vma=False,
    )
```

```python
import functools

import jax
import jax.numpy as jnp
from jax import lax
from jax.experimental import pallas as pl
from jax.experimental.pallas import tpu as pltpu
from jax.sharding import PartitionSpec as P

BS = 128
MIB = 1 << 20
ROW_BY_ROW = (((1,), (1,)), ((), ()))
BY_TOKEN = (((0,), (0,)), ((), ()))
VMEM = pl.BlockSpec(memory_space=pltpu.VMEM)
SMEM = pl.BlockSpec(memory_space=pltpu.SMEM)
HBM = pl.BlockSpec(memory_space=pltpu.HBM)


def dot(a, b, dims=(((1,), (0,)), ((), ()))):
    return lax.dot_general(a, b, dims, preferred_element_type=jnp.float32)


def load_kernel(start, w_hbm, out_ref, sem):
    copy, _ = start_copies(w_hbm, start, out_ref, sem)

    def finish(i, carry):
        copy(i).wait()
        return carry

    lax.fori_loop(0, sem.shape[0], finish, 0)


def in_hbm(value):
    return pltpu.with_memory_space_constraint(value, pltpu.HBM)


def load(weight, start, rows):
    chunks = 1
    return pl.pallas_call(
        functools.partial(load_kernel, start),
        out_shape=pltpu.VMEM((rows, weight.shape[1]), weight.dtype),
        in_specs=[HBM],
        out_specs=VMEM,
        scratch_shapes=[pltpu.SemaphoreType.DMA((chunks,))],
        compiler_params=pltpu.CompilerParams(vmem_limit_bytes=MIB),
    )(in_hbm(weight))


def add_blocks(acc, source, deltas, m, model, hidden, live, transposed):
    blocks = acc.shape[1] // BS
    for s in range(deltas.shape[1]):
        at_m = pl.ds(pl.multiple_of(model[m, s] * BS, BS), BS)
        at_h = pl.ds(pl.multiple_of(lax.rem(hidden[m, s], blocks) * BS, BS), BS)
        active = jnp.where(s < live[m], deltas[m, s], jnp.zeros_like(deltas[m, s]))
        if transposed:
            acc[:, at_h] += dot(source[:, at_m], active, ROW_BY_ROW)
        else:
            acc[:, at_h] += dot(source[:, at_m], active)


def start_copies(source, start, target, sem):
    step = target.shape[0] // sem.shape[0]

    def copy(i):
        at = pl.multiple_of(i * step, step)
        return pltpu.make_async_copy(
            source.at[pl.ds(start + at, step)], target.at[pl.ds(at, step)], sem.at[i]
        )

    def begin(i, carry):
        copy(i).start()
        return carry

    lax.fori_loop(0, sem.shape[0], begin, 0)
    return copy, step


def forward_kernel(
    mine, theirs, g_lo, g_hi, u_lo, w_up, w_down, deltas, model, hidden, live,
    x_ref, dy_ref, activ_ref, up_ref, gate_ref, u_hi, gate_acc, up_acc, act_acc, d_part, u_sem, sem,
):
    u_copy, _ = start_copies(w_up, w_up.shape[0] - u_hi.shape[0], u_hi, u_sem)
    copy, step = start_copies(w_down, 0, d_part, sem)
    half, width = mine.shape[0], x_ref.shape[1]
    depth = g_lo.shape[0]
    x_ref[0:half, :] = mine[:, 0:width]
    x_ref[half:, :] = theirs[:, 0:width]
    dy_ref[0:half, :] = mine[:, width:]
    dy_ref[half:, :] = theirs[:, width:]
    gate_acc[...] = dot(x_ref[:, 0:depth], g_lo[...])
    gate_acc[...] += dot(x_ref[:, depth:], g_hi[...])
    up_acc[...] = dot(x_ref[:, 0:depth], u_lo[...])
    for i in range(u_sem.shape[0]):
        u_copy(i).wait()
    up_acc[...] += dot(x_ref[:, depth:], u_hi[...])
    add_blocks(gate_acc, x_ref, deltas, 0, model, hidden, live, False)
    add_blocks(up_acc, x_ref, deltas, 1, model, hidden, live, False)

    def down(i, carry):
        copy(i).wait()
        at = pl.ds(pl.multiple_of(i * step, step), step)
        act_acc[:, at] = dot(d_part[at, :], dy_ref[...], ROW_BY_ROW).T
        return carry

    lax.fori_loop(0, sem.shape[0], down, 0)
    add_blocks(act_acc, dy_ref, deltas, 2, model, hidden, live, True)
    gate, up, grad_act = gate_acc[...], up_acc[...], act_acc[...]
    sigma = jax.nn.sigmoid(gate)
    silu_gate = gate * sigma
    activ_ref[...] = (silu_gate * up).astype(jnp.bfloat16)
    up_ref[...] = (grad_act * silu_gate).astype(jnp.bfloat16)
    gate_ref[...] = (grad_act * up * sigma * (1.0 + gate * (1.0 - sigma))).astype(jnp.bfloat16)


def backward_kernel(
    start, grad_gate, grad_up, g_part, u_part, deltas, model, hidden, live, keep_ref, send_ref, acc
):
    slots = deltas.shape[1]
    blocks = grad_gate.shape[1] // BS
    columns = g_part.shape[0]
    half = keep_ref.shape[0]
    tall = min(1024, columns)
    for i in range(0, columns, tall):
        total = dot(g_part[i : i + tall, :], grad_gate[...], ROW_BY_ROW)
        total += dot(u_part[i : i + tall, :], grad_up[...], ROW_BY_ROW)
        acc[:, i : i + tall] = total.T
    for m, grad in ((0, grad_gate), (1, grad_up)):
        for s in range(slots):
            column = model[m, s] * BS - start
            inside = (s < live[m]) & (column >= 0) & (column < columns)
            at_m = pl.ds(pl.multiple_of(jnp.clip(column, 0, columns - BS), BS), BS)
            at_h = pl.ds(pl.multiple_of(lax.rem(hidden[m, s], blocks) * BS, BS), BS)
            active = jnp.where(inside, deltas[m, s], jnp.zeros_like(deltas[m, s]))
            acc[:, at_m] += dot(grad[:, at_h], active, ROW_BY_ROW)

    keep_ref[...] = acc[0:half, :]
    send_ref[...] = acc[half:, :].astype(jnp.bfloat16)


def moments_kernel(
    x_rows, dy_rows, activ, grad_up, grad_gate, model, hidden, live, mean, square, mean_out, square_out
):
    slots = mean.shape[1]
    blocks = activ.shape[1] // BS
    for m, grad in ((0, grad_gate), (1, grad_up), (2, activ)):

        @pl.when(pl.program_id(0) == m)
        def _(m=m, grad=grad):
            for s in range(slots):
                at_h = pl.ds(pl.multiple_of(lax.rem(hidden[m, s], blocks) * BS, BS), BS)
                at_m = pl.ds(pl.multiple_of(model[m, s] * BS, BS), BS)
                if m == 2:
                    block = dot(grad[:, at_h], dy_rows[:, at_m], BY_TOKEN)
                else:
                    block = dot(x_rows[:, at_m], grad[:, at_h], BY_TOKEN)
                keep = s < live[m]
                old_mean, old_square = mean[0, s], square[0, s]
                mean_out[0, s] = jnp.where(keep, 0.9 * old_mean + 0.1 * block, old_mean)
                square_out[0, s] = jnp.where(
                    keep, 0.999 * old_square + 0.001 * block * block, old_square
                )


def stack(first, second, axis):
    zero = jnp.zeros((), first.dtype)
    after = [(0, 0, 0), (0, 0, 0)]
    before = [(0, 0, 0), (0, 0, 0)]
    after[axis] = (0, second.shape[axis], 0)
    before[axis] = (first.shape[axis], 0, 0)
    return lax.pad(first, zero, after) + lax.pad(second, zero, before)


def per_device(
    devices,
    tokens,
    out_grad,
    w_gate,
    w_up,
    w_down,
    deltas,
    model_block,
    hidden_block,
    live_count,
    prior_mean,
    prior_square,
):
    width, wide = w_gate.shape
    bits = [1 << k for k in range(devices.bit_length() - 1)]
    count = tokens.shape[0] * devices
    half = count // 2
    part = width // 2
    f32, bf16 = jnp.float32, jnp.bfloat16

    def swap(value, bit):
        return lax.ppermute(value, "tensor", [(i, i ^ bit) for i in range(devices)])

    live = live_count.reshape(-1)
    positions = (model_block, hidden_block, live)
    near, far = bits[:-2], bits[-2:]
    straight = [far[1], far[0], far[0] ^ far[1]]
    held = stack(tokens, out_grad, 1)
    came = [swap(held, bit) for bit in straight]
    held = jnp.concatenate([held] + came, axis=0)
    for bit in near[:0:-1]:
        held = stack(held, swap(held, bit), 0)
    other = swap(held, bits[0])
    g_parts = [load(w_gate, i * part, part) for i in range(2)]
    u_lo = load(w_up, 0, part)

    x_rows, dy_rows, activ, grad_up, grad_gate, u_hi = pl.pallas_call(
        forward_kernel,
        out_shape=(
            jax.ShapeDtypeStruct((count, width), bf16),
            jax.ShapeDtypeStruct((count, width), bf16),
            jax.ShapeDtypeStruct((count, wide), bf16),
            jax.ShapeDtypeStruct((count, wide), bf16),
            jax.ShapeDtypeStruct((count, wide), bf16),
            pltpu.VMEM((part, wide), bf16),
        ),
        in_specs=[VMEM] * 5 + [HBM, HBM, VMEM] + [SMEM] * 3,
        out_specs=[VMEM] * 6,
        scratch_shapes=[
            pltpu.VMEM((count, wide), f32),
            pltpu.VMEM((count, wide), f32),
            pltpu.VMEM((count, wide), f32),
            pltpu.VMEM(w_down.shape, bf16),
            pltpu.SemaphoreType.DMA((2,)),
            pltpu.SemaphoreType.DMA((max(1, min(2, wide // BS)),)),
        ],
        compiler_params=pltpu.CompilerParams(vmem_limit_bytes=19 * MIB),
        name="forward",
    )(
        held, other, *g_parts, u_lo, in_hbm(w_up), in_hbm(w_down), deltas, *positions
    )

    u_parts = (u_lo, u_hi)
    pieces = []
    for i in range(2):
        keep, send = pl.pallas_call(
            functools.partial(backward_kernel, i * part),
            out_shape=(
                jax.ShapeDtypeStruct((half, part), f32),
                jax.ShapeDtypeStruct((half, part), bf16),
            ),
            in_specs=[VMEM] * 5 + [SMEM] * 3,
            out_specs=[VMEM] * 2,
            scratch_shapes=[pltpu.VMEM((count, part), f32)],
            compiler_params=pltpu.CompilerParams(vmem_limit_bytes=8 * MIB),
        )(grad_gate, grad_up, g_parts[i], u_parts[i], deltas, *positions)
        pieces.append(keep + swap(send, bits[0]).astype(f32))
    left = half // 2
    keep = stack(pieces[0][:left], pieces[1][:left], 1)
    send = stack(pieces[0][left:], pieces[1][left:], 1).astype(bf16)
    for bit in near[1:]:
        total = keep + swap(send, bit).astype(f32)
        left = total.shape[0] // 2
        keep, send = total[:left], total[left:].astype(bf16)
    rows = tokens.shape[0]
    input_grad = total[:rows]
    for k, bit in enumerate(straight, 1):
        send = total[k * rows : (k + 1) * rows].astype(bf16)
        input_grad += swap(send, bit).astype(f32)
    input_grad = input_grad.astype(bf16)

    slots = deltas.shape[1]
    block = pl.BlockSpec((1, slots, BS, BS), lambda m: (m, 0, 0, 0))
    mean, square = pl.pallas_call(
        moments_kernel,
        grid=(3,),
        out_shape=(
            jax.ShapeDtypeStruct(prior_mean.shape, f32),
            jax.ShapeDtypeStruct(prior_square.shape, f32),
        ),
        in_specs=[VMEM] * 5 + [SMEM] * 3 + [block] * 2,
        out_specs=[block] * 2,
        compiler_params=pltpu.CompilerParams(vmem_limit_bytes=8 * MIB),
        name="moments",
    )(x_rows, dy_rows, activ, grad_up, grad_gate, *positions, prior_mean, prior_square)
    return input_grad, mean, square


def solution(mesh):
    placed = (
        P(("groups", "tensor"), None),
        P(("groups", "tensor"), None),
        P(None, "tensor"),
        P(None, "tensor"),
        P("tensor", None),
        P("groups", "tensor", None, None),
        P("groups", "tensor"),
        P("groups", "tensor"),
        P("groups", "tensor"),
        P("groups", "tensor", None, None),
        P("groups", "tensor", None, None),
    )
    devices = mesh.shape["tensor"]
    return jax.shard_map(
        functools.partial(per_device, devices),
        mesh=mesh,
        in_specs=placed,
        out_specs=(
            P(("groups", "tensor"), None),
            P("groups", "tensor", None, None),
            P("groups", "tensor", None, None),
        ),
        check_vma=False,
    )
```
